32 devices in a mesh: rep: 4 (over z), exp: 8 (over y, x, core).
Axes of the slice: x: 2, y: 2, z: 4, core: 2. Of those that a mesh axis runs over, the one named last changes fastest.
Arguments:
- tokens: bfloat16 [1536, 2048], P(('rep', 'exp')), may hold values from -6 to 6
- grad_out: bfloat16 [1536, 2048], P(('rep', 'exp')), may hold values from -6 to 6
- expert_ids: int32 [1536, 8], P(('rep', 'exp')), may hold values from 0 to 15, all different within a row; in each aligned block of 48 rows (0 to 47, 48 to 95, ...) at most 26 rows name the same one
- gate_probs: float32 [1536, 8], P(('rep', 'exp')), may hold values from 0.05 to 1
- gate_weight: bfloat16 [32, 2048, 384], P(('rep', 'exp')), may hold values from -0.125 to 0.125
- up_weight: bfloat16 [32, 2048, 384], P(('rep', 'exp')), may hold values from -0.125 to 0.125
- down_weight: bfloat16 [32, 384, 2048], P(('rep', 'exp')), may hold values from -0.21875 to 0.21875
Outputs:
- token_grad: bfloat16 [1536, 2048], P(('rep', 'exp'))
- gate_grad: bfloat16 [32, 2048, 384], P(('rep', 'exp'))
- up_grad: bfloat16 [32, 2048, 384], P(('rep', 'exp'))
- down_grad: bfloat16 [32, 384, 2048], P(('rep', 'exp'))
The draws below stay inside these ranges and needn't reach their ends.
Inputs may be any that keep to these rules, and one draw needn't show every extreme that they name: `expert_ids`: the 8 experts of a token are distinct; among the 48 tokens of one device no expert is chosen more than 26 times, and that many in some device.
All inputs are finite; a program needn't handle non-finite values.
Results may differ from the reference program's by a relative error of at most 0.0058.
Values may be sent and summed in bfloat16 or wider, within the bound.
No kernel may reach another device: no remote copies, remote signals or barrier semaphores. Data moves between devices by JAX's collectives and lax.ppermute only.
A program may use at most 128 MiB of HBM per device.

```python
import math
import jax
import jax.numpy as jnp
import numpy as np
from jax import lax

D = 2048
FF = 768
TOP = 8
TOK_DEV = 48
EXPERTS = 16
CAP = 26
TOKENS = 1536
SLOTS = 832


def block_scale(key, extent, split, low, top_value):
    gain = 1.0
    for dim, shards_of in split:
        steps = jax.random.uniform(jax.random.fold_in(jax.random.fold_in(key, 6), dim), (shards_of,), jnp.float32, low / len(split), top_value / len(split))
        gain = gain * jnp.repeat(jnp.exp(steps), extent[dim] // shards_of).reshape((-1,) + (1,) * (len(extent) - 1 - dim))
    return gain


def routed_block(key, own, number, rows, count, top, reach, slope):
    order = jax.random.permutation(key, count)
    heavy_load, common = portions_of(count, rows * top, reach, slope, True), portions_of(count, rows * top, reach, slope, False)
    places = jnp.arange(count)

    def named(lengths, turn):
        used = int((lengths > 0).sum())
        fixed = max(1, used // 4)
        shifted = fixed + (places - fixed + turn * (used - fixed)) % max(1, count - fixed)
        return jnp.zeros((count,), jnp.int32).at[order[jnp.where(places < fixed, places, shifted)]].set(jnp.asarray(lengths, jnp.int32))

    lengths = jnp.where(number % 4 == 0, named(heavy_load, number // 4), named(common, number - number // 4 - 1))
    mixed = jax.random.permutation(jax.random.fold_in(own, 3), count)
    donor, sink = mixed[0:count // 2 * 2:2], mixed[1:count // 2 * 2:2]
    margin = jnp.minimum(lengths[donor] - 1, reach - lengths[sink]) // 2
    margin = jnp.where((donor == order[0]) | (sink == order[0]) | (lengths[sink] == 0), 0, jnp.maximum(margin, 0))
    shifted = jax.random.randint(jax.random.fold_in(own, 4), (count // 2,), 0, 1 << 20) % (margin + 1)
    lengths = lengths.at[donor].add(-shifted).at[sink].add(shifted)
    members = jnp.searchsorted(jnp.cumsum(lengths), jnp.arange(rows * top), side="right").astype(jnp.int32)
    table = members.reshape(top, rows).T
    table = table[jax.random.permutation(jax.random.fold_in(own, 1), rows)]
    turn = jax.random.randint(jax.random.fold_in(own, 2), (rows, 1), 0, top)
    return jnp.take_along_axis(table, (jnp.arange(top)[None, :] + turn) % top, axis=1)


def portions_of(count, total, bound, lean, full):
    loads = [(1 << 20) // math.isqrt(rank ** lean) + 1 for rank in range(1, count + 1)]
    largest = bound if full else min(bound, max(-(-total // count), total * loads[0] // sum(loads)))
    least = 1 if total - largest >= count - 1 else 0
    counts, spare = [largest] + [least] * (count - 1), total - largest - least * (count - 1)
    while spare > 0:
        free = [i for i in range(1, count) if counts[i] < largest] or [i for i in range(1, count) if counts[i] < bound]
        pool, left = sum([loads[i] for i in free]), spare
        for i in free:
            extra = min(bound - counts[i], max(1, left * loads[i] // pool), spare)
            counts[i] = counts[i] + extra
            spare = spare - extra
    return np.array(counts)


def scatter_about(own_key, shape, width, bound, split=(), kind=jnp.bfloat16):
    drawn = jax.random.normal(own_key, shape, jnp.float32) * width
    if len(split) > 0:
        drawn = block_scale(own_key, shape, split, -0.22, 0.18) * drawn
    return jnp.clip(drawn, min=-bound, max=bound).astype(kind)


def setup_inputs(seed: int = 0) -> dict:
    splits = jax.random.split(jax.random.key(seed), 8)
    tokens = scatter_about(splits[0], (TOKENS, D), 1.0, 6.0, ((0, 32),))
    grad_out = scatter_about(splits[1], (TOKENS, D), 1.0, 6.0, ((0, 32),))
    expert_ids_keys = jax.random.split(jax.random.fold_in(splits[2], 1), TOKENS // TOK_DEV)
    expert_ids_turns = jax.random.permutation(jax.random.fold_in(splits[2], 3), TOKENS // TOK_DEV)
    expert_ids = jax.vmap(lambda own, number: routed_block(jax.random.fold_in(splits[2], 2), own, number, TOK_DEV, EXPERTS, TOP, CAP, 2))(expert_ids_keys, expert_ids_turns).reshape((TOKENS, TOP))
    gate_probs = jnp.clip(0.05 + 0.95 * jax.random.uniform(splits[3], (TOKENS, TOP), jnp.float32) ** block_scale(splits[3], (TOKENS, TOP), ((0, 32),), -0.2, 0.2), 0.05, 1.0)
    gate_weight = scatter_about(splits[4], (2 * EXPERTS, D, FF // 2), D ** -0.5, 0.125, ((0, 32),))
    up_weight = scatter_about(splits[5], (2 * EXPERTS, D, FF // 2), D ** -0.5, 0.125, ((0, 32),))
    down_weight = scatter_about(splits[6], (2 * EXPERTS, FF // 2, D), FF ** -0.5, 0.21875, ((0, 32),))
    return {"tokens": tokens, "grad_out": grad_out, "expert_ids": expert_ids, "gate_probs": gate_probs, "gate_weight": gate_weight, "up_weight": up_weight, "down_weight": down_weight}


def reference(tokens, grad_out, expert_ids, gate_probs, gate_weight, up_weight, down_weight):
    half = FF // 2
    gate_full = gate_weight.reshape(EXPERTS, 2, D, half).transpose(0, 2, 1, 3).reshape(EXPERTS, D, FF)
    up_full = up_weight.reshape(EXPERTS, 2, D, half).transpose(0, 2, 1, 3).reshape(EXPERTS, D, FF)
    down_full = down_weight.reshape(EXPERTS, FF, D)
    flat_ids = expert_ids.reshape(-1)
    flat_probs = gate_probs.reshape(-1)

    def expert_step(accumulated, inputs):
        expert_index, gate_mat, up_mat, down_mat = inputs
        matches = flat_ids == expert_index
        positions = jnp.nonzero(matches, size=SLOTS, fill_value=0)[0].astype(jnp.int32)
        match_count = jnp.sum(matches.astype(jnp.int32))
        validity = (jnp.arange(SLOTS, dtype=jnp.int32) < match_count).astype(jnp.float32)
        token_ids = (positions // TOP).astype(jnp.int32)
        rows_in = (tokens[token_ids].astype(jnp.float32) * validity[:, None]).astype(jnp.bfloat16)
        rows_grad = (flat_probs[positions][:, None] * grad_out[token_ids].astype(jnp.float32) * validity[:, None]).astype(jnp.bfloat16)
        gate_pre = jnp.dot(rows_in, gate_mat, preferred_element_type=jnp.float32)
        up_pre = jnp.dot(rows_in, up_mat, preferred_element_type=jnp.float32)
        sigmoid_gate = jax.nn.sigmoid(gate_pre)
        activated = gate_pre * sigmoid_gate
        hidden = (activated * up_pre).astype(jnp.bfloat16)
        hidden_grad = jnp.dot(rows_grad, down_mat.T, preferred_element_type=jnp.float32)
        up_in = (hidden_grad * activated).astype(jnp.bfloat16)
        gate_in = (hidden_grad * up_pre * sigmoid_gate * (1.0 + gate_pre * (1.0 - sigmoid_gate))).astype(jnp.bfloat16)
        contrib = jnp.dot(gate_in, gate_mat.T, preferred_element_type=jnp.float32) + jnp.dot(up_in, up_mat.T, preferred_element_type=jnp.float32)
        accumulated = accumulated.at[token_ids].add(contrib * validity[:, None])
        grad_gate = jnp.dot(rows_in.T, gate_in, preferred_element_type=jnp.float32).astype(jnp.bfloat16)
        grad_up = jnp.dot(rows_in.T, up_in, preferred_element_type=jnp.float32).astype(jnp.bfloat16)
        grad_down = jnp.dot(hidden.T, rows_grad, preferred_element_type=jnp.float32).astype(jnp.bfloat16)
        return accumulated, (grad_gate, grad_up, grad_down)

    start = jnp.zeros((TOKENS, D), jnp.float32)
    indices = jnp.arange(EXPERTS, dtype=jnp.int32)
    accumulated, stacked = lax.scan(expert_step, start, (indices, gate_full, up_full, down_full))
    grad_gate, grad_up, grad_down = stacked
    gate_grad = grad_gate.reshape(EXPERTS, D, 2, half).transpose(0, 2, 1, 3).reshape(2 * EXPERTS, D, half)
    up_grad = grad_up.reshape(EXPERTS, D, 2, half).transpose(0, 2, 1, 3).reshape(2 * EXPERTS, D, half)
    down_grad = grad_down.reshape(2 * EXPERTS, half, D)
    return (accumulated.astype(jnp.bfloat16), gate_grad, up_grad, down_grad)
```

```python
import jax
import jax.numpy as jnp
from jax import lax
from jax.sharding import PartitionSpec as P


AXES = ("rep", "exp")


def flip_pairs(move):
    pairs = []
    for z in range(4):
        for y in range(2):
            for x in range(2):
                for c in range(2):
                    tz, ty, tx, tc = move(z, y, x, c)
                    pairs.append((((z * 2 + y) * 2 + x) * 2 + c, ((tz * 2 + ty) * 2 + tx) * 2 + tc))
    return pairs


OTHER_CORE = flip_pairs(lambda z, y, x, c: (z, y, x, 1 - c))
FIRST_FLIP = flip_pairs(lambda z, y, x, c: (z, y, 1 - x, c) if c == 0 else (z, 1 - y, x, c))
SECOND_FLIP = flip_pairs(lambda z, y, x, c: (z, 1 - y, x, c) if c == 0 else (z, y, 1 - x, c))
Z_FLIP = {
    1: flip_pairs(lambda z, y, x, c: (z ^ 1, y, x, c)),
    2: flip_pairs(lambda z, y, x, c: (z ^ 2, y, x, c)),
    3: flip_pairs(lambda z, y, x, c: (z ^ 3, y, x, c)),
}
LAST = (((1,), (1,)), ((), ()))
FIRST = (((0,), (0,)), ((), ()))


def move(value, pairs):
    return lax.ppermute(value, AXES, pairs)


def dense_device(tokens, grad_out, expert_ids, gate_probs, gate_weight, up_weight, down_weight):
    rows, features = tokens.shape
    experts = lax.axis_size("rep") * lax.axis_size("exp") // 2
    half = gate_weight.shape[2]
    mine = (lax.axis_index("rep") * lax.axis_size("exp") + lax.axis_index("exp")) // 2
    f32, b16 = jnp.float32, jnp.bfloat16

    gate_other = move(gate_weight[0], OTHER_CORE)
    up_other = move(up_weight[0], OTHER_CORE)
    down_other = move(down_weight[0], OTHER_CORE)
    in_mat = jnp.concatenate([gate_weight[0], gate_other, up_weight[0], up_other], axis=1)
    down_mat = jnp.concatenate([down_weight[0], down_other], axis=0)

    chosen = expert_ids[:, :, None] == jnp.arange(experts, dtype=jnp.int32)
    dense = jnp.sum(jnp.where(chosen, gate_probs[:, :, None], 0.0), axis=1)
    high = lax.reduce_precision(dense, 8, 7)
    middle = lax.reduce_precision(dense - high, 8, 7)
    low = dense - high - middle
    terms = jnp.concatenate([high, middle, low], axis=1).astype(b16)
    pad = -terms.shape[1] % 128
    block = jnp.concatenate([tokens, grad_out, jnp.pad(terms, ((0, 0), (0, pad)))], axis=1)
    lanes = jnp.arange(3 * experts + pad, dtype=jnp.int32)
    wanted = (lanes < 3 * experts) & (lanes % experts == mine)

    ins, inner, hiddens, scaleds, totals = [], [], [], [], []
    for step in range(4):
        own = block if step == 0 else move(block, Z_FLIP[step])
        first = move(own, FIRST_FLIP)
        chunk = jnp.concatenate([own, first, move(own, SECOND_FLIP), move(first, SECOND_FLIP)], axis=0)
        rows_in = chunk[:, :features]
        weight = jnp.sum(jnp.where(wanted, chunk[:, 2 * features :].astype(f32), 0.0), axis=1, keepdims=True)
        scaled = (weight * chunk[:, features : 2 * features].astype(f32)).astype(b16)
        pre = jnp.dot(rows_in, in_mat, preferred_element_type=f32)
        gate_pre, up_pre = pre[:, : 2 * half], pre[:, 2 * half :]
        hidden_grad = lax.dot_general(scaled, down_mat, LAST, preferred_element_type=f32)
        sigmoid_gate = jax.nn.sigmoid(gate_pre)
        activated = gate_pre * sigmoid_gate
        hidden = (activated * up_pre).astype(b16)
        up_in = (hidden_grad * activated).astype(b16)
        gate_in = (hidden_grad * up_pre * sigmoid_gate * (1.0 + gate_pre * (1.0 - sigmoid_gate))).astype(b16)
        both_in = jnp.concatenate([gate_in, up_in], axis=1)
        partial = lax.dot_general(both_in, in_mat, LAST, preferred_element_type=f32)
        partial = partial[: 2 * rows] + move(partial[2 * rows :].astype(b16), SECOND_FLIP).astype(f32)
        partial = partial[:rows] + move(partial[rows:].astype(b16), FIRST_FLIP).astype(f32)
        if step > 0:
            partial = move(partial.astype(b16), Z_FLIP[step]).astype(f32)
        totals.append(partial)
        ins.append(rows_in)
        inner.append(both_in)
        hiddens.append(hidden)
        scaleds.append(scaled)
    token_grad = (totals[0] + totals[1] + totals[2] + totals[3]).astype(b16)

    all_in = jnp.concatenate(ins, axis=0)
    all_inner = jnp.concatenate(inner, axis=0)
    all_hidden = jnp.concatenate(hiddens, axis=0)
    all_scaled = jnp.concatenate(scaleds, axis=0)

    def grads(part):
        gate = lax.dot_general(all_in, all_inner[:, part * half : (part + 1) * half], FIRST, preferred_element_type=f32)
        up = lax.dot_general(all_in, all_inner[:, (2 + part) * half : (3 + part) * half], FIRST, preferred_element_type=f32)
        down = lax.dot_general(all_hidden[:, part * half : (part + 1) * half], all_scaled, FIRST, preferred_element_type=f32)
        return gate, up, down

    arrived = [move(value.astype(b16), OTHER_CORE) for value in grads(1)]
    summed = [(here + there.astype(f32)).astype(b16)[None] for here, there in zip(grads(0), arrived)]
    return (token_grad, *summed)


def sparse_device(tokens, grad_out, expert_ids, gate_probs, gate_weight, up_weight, down_weight):
    rep_count = lax.axis_size("rep")
    exp_count = lax.axis_size("exp")
    tok_rows, features = tokens.shape
    top_count = expert_ids.shape[1]
    experts = rep_count * exp_count // 2
    capacity = 2 * ((tok_rows * top_count // experts + 2) // 2)
    routed = tok_rows * top_count
    flat_ids = expert_ids.reshape(routed)
    order_index = jnp.arange(routed, dtype=jnp.int32)
    earlier = (flat_ids[:, None] == flat_ids[None, :]) & (
        order_index[None, :] < order_index[:, None]
    )
    slot_rank = jnp.sum(earlier.astype(jnp.int32), axis=1)
    slot_index = flat_ids * capacity + slot_rank
    slot_range = jnp.arange(experts * capacity, dtype=jnp.int32)
    selector = slot_range[:, None] == slot_index[None, :]
    select_rows = selector.astype(jnp.bfloat16)
    rows_in = jnp.repeat(tokens, top_count, axis=0)
    rows_grad = (
        (gate_probs[:, :, None] * grad_out[:, None, :].astype(jnp.float32))
        .reshape(routed, features)
        .astype(jnp.bfloat16)
    )
    packed_in = jnp.dot(select_rows, rows_in, preferred_element_type=jnp.float32).astype(
        jnp.bfloat16
    )
    packed_grad = jnp.dot(select_rows, rows_grad, preferred_element_type=jnp.float32).astype(
        jnp.bfloat16
    )
    send_in = jnp.repeat(packed_in.reshape(experts, capacity, features), 2, axis=0).reshape(
        rep_count, exp_count, capacity, features
    )
    send_grad = jnp.repeat(packed_grad.reshape(experts, capacity, features), 2, axis=0).reshape(
        rep_count, exp_count, capacity, features
    )
    recv_in, recv_grad = (
        lax.all_to_all(
            lax.all_to_all(send_in, "rep", split_axis=0, concat_axis=0, tiled=True),
            "exp",
            split_axis=1,
            concat_axis=1,
            tiled=True,
        ),
        lax.all_to_all(
            lax.all_to_all(send_grad, "rep", split_axis=0, concat_axis=0, tiled=True),
            "exp",
            split_axis=1,
            concat_axis=1,
            tiled=True,
        ),
    )
    slots = rep_count * exp_count * capacity
    slot_in = recv_in.reshape(slots, features)
    slot_grad = recv_grad.reshape(slots, features)
    gate_mat = gate_weight[0]
    up_mat = up_weight[0]
    down_mat = down_weight[0]
    contract_last = (((1,), (1,)), ((), ()))
    contract_first = (((0,), (0,)), ((), ()))
    gate_pre = jnp.dot(slot_in, gate_mat, preferred_element_type=jnp.float32)
    up_pre = jnp.dot(slot_in, up_mat, preferred_element_type=jnp.float32)
    sigmoid_gate = jax.nn.sigmoid(gate_pre)
    activated = gate_pre * sigmoid_gate
    hidden = (activated * up_pre).astype(jnp.bfloat16)
    hidden_grad = lax.dot_general(
        slot_grad, down_mat, contract_last, preferred_element_type=jnp.float32
    )
    up_in = (hidden_grad * activated).astype(jnp.bfloat16)
    gate_in = (
        hidden_grad * up_pre * sigmoid_gate * (1.0 + gate_pre * (1.0 - sigmoid_gate))
    ).astype(jnp.bfloat16)
    partial_rows = lax.dot_general(
        gate_in, gate_mat, contract_last, preferred_element_type=jnp.float32
    ) + lax.dot_general(up_in, up_mat, contract_last, preferred_element_type=jnp.float32)
    gate_grad = lax.dot_general(
        slot_in, gate_in, contract_first, preferred_element_type=jnp.float32
    ).astype(jnp.bfloat16)[None]
    up_grad = lax.dot_general(
        slot_in, up_in, contract_first, preferred_element_type=jnp.float32
    ).astype(jnp.bfloat16)[None]
    down_grad = lax.dot_general(
        hidden, slot_grad, contract_first, preferred_element_type=jnp.float32
    ).astype(jnp.bfloat16)[None]
    partial_grid = partial_rows.reshape(rep_count, exp_count, capacity, features)
    returned_grid = lax.all_to_all(
        lax.all_to_all(partial_grid, "rep", split_axis=0, concat_axis=0, tiled=True),
        "exp",
        split_axis=1,
        concat_axis=1,
        tiled=True,
    )
    returned = jnp.sum(returned_grid.reshape(experts, 2, capacity, features), axis=1).reshape(
        experts * capacity, features
    )
    routed_grads = returned[slot_index]
    token_grad = jnp.sum(routed_grads.reshape(tok_rows, top_count, features), axis=1).astype(
        jnp.bfloat16
    )
    return (token_grad, gate_grad, up_grad, down_grad)


def per_device(tokens, grad_out, expert_ids, *rest):
    experts = lax.axis_size("rep") * lax.axis_size("exp") // 2
    if lax.axis_size("rep") == 4 and lax.axis_size("exp") == 8 and 2 * expert_ids.shape[1] >= experts:
        return dense_device(tokens, grad_out, expert_ids, *rest)
    return sparse_device(tokens, grad_out, expert_ids, *rest)


def solution(mesh):
    return jax.shard_map(
        per_device,
        mesh=mesh,
        in_specs=(
            P(("rep", "exp"), None),
            P(("rep", "exp"), None),
            P(("rep", "exp"), None),
            P(("rep", "exp"), None),
            P(("rep", "exp"), None, None),
            P(("rep", "exp"), None, None),
            P(("rep", "exp"), None, None),
        ),
        out_specs=(
            P(("rep", "exp"), None),
            P(("rep", "exp"), None, None),
            P(("rep", "exp"), None, None),
            P(("rep", "exp"), None, None),
        ),
        check_vma=False,
    )
```

```python
import functools

import jax
import jax.numpy as jnp
from jax import lax
from jax.experimental import pallas as pl
from jax.experimental.pallas import tpu as pltpu
from jax.sharding import PartitionSpec as P


AXES = ("rep", "exp")


def flip_pairs(move):
    pairs = []
    for z in range(4):
        for y in range(2):
            for x in range(2):
                for c in range(2):
                    tz, ty, tx, tc = move(z, y, x, c)
                    pairs.append((((z * 2 + y) * 2 + x) * 2 + c, ((tz * 2 + ty) * 2 + tx) * 2 + tc))
    return pairs


OTHER_CORE = flip_pairs(lambda z, y, x, c: (z, y, x, 1 - c))
FIRST_FLIP = flip_pairs(lambda z, y, x, c: (z, y, 1 - x, c) if c == 0 else (z, 1 - y, x, c))
SECOND_FLIP = flip_pairs(lambda z, y, x, c: (z, 1 - y, x, c) if c == 0 else (z, y, 1 - x, c))
SHIFTS = (0, 3, 2, 1)
Z_IN = [flip_pairs(lambda z, y, x, c, s=s: ((z - s) % 4, y, x, c)) for s in SHIFTS]
Z_BACK = [flip_pairs(lambda z, y, x, c, s=s: ((z + s) % 4, y, x, c)) for s in SHIFTS]
LAST = (((1,), (1,)), ((), ()))
FIRST = (((0,), (0,)), ((), ()))
F32, B16 = jnp.float32, jnp.bfloat16


def move(value, pairs):
    return lax.ppermute(value, AXES, pairs)


def chunk_kernel(features, half, rows, *refs):
    wanted, blocks, in_mat, down_mat = refs[0], refs[1:5], refs[5], refs[6]
    rows_out, scaled_out, gate_out, up_out, hidden_out, keep, send = refs[-8:-1]
    total = refs[-1]
    step = pl.program_id(0)

    @pl.when(step == 0)
    def _():
        for i, block in enumerate(blocks):
            place = pl.ds(i * rows, rows)
            rows_out[place, :] = block[:, :features]
            terms = jnp.where(wanted[...] > 0.0, block[:, 2 * features :].astype(F32), 0.0)
            weight = jnp.sum(terms, axis=1, keepdims=True)
            scaled_out[place, :] = (weight * block[:, features : 2 * features].astype(F32)).astype(B16)

    pre = jnp.dot(rows_out[...], in_mat[0], preferred_element_type=F32)
    gate_pre, up_pre = pre[:, :half], pre[:, half:]
    hidden_grad = lax.dot_general(scaled_out[...], down_mat[0], LAST, preferred_element_type=F32)
    sigmoid_gate = jax.nn.sigmoid(gate_pre)
    activated = gate_pre * sigmoid_gate
    hidden_out[0] = (activated * up_pre).astype(B16)
    up_in = (hidden_grad * activated).astype(B16)
    gate_in = (hidden_grad * up_pre * sigmoid_gate * (1.0 + gate_pre * (1.0 - sigmoid_gate))).astype(B16)
    gate_out[0] = gate_in
    up_out[0] = up_in
    part = lax.dot_general(jnp.concatenate([gate_in, up_in], axis=1), in_mat[0], LAST, preferred_element_type=F32)

    @pl.when(step == 0)
    def _():
        total[...] = part

    @pl.when(step == 1)
    def _():
        keep[...] = total[: 2 * rows, :] + part[: 2 * rows]
        send[...] = (total[2 * rows :, :] + part[2 * rows :]).astype(B16)


def chunk_call(place, chunks, wanted, blocks, in_mats, down_mats, stacks):
    rows, width = blocks[0].shape
    features = down_mats.shape[2]
    half = down_mats.shape[1]
    many = 4 * rows
    whole = lambda shape: pl.BlockSpec(shape, lambda j: (0,) * len(shape))
    wide = pl.BlockSpec((many, features), lambda j: (place, 0))
    thin = pl.BlockSpec((1, many, half), lambda j: (j, place, 0))
    in_specs = [whole(wanted.shape)] + [whole((rows, width))] * 4 + [
        pl.BlockSpec((1,) + in_mats.shape[1:], lambda j: (j, 0, 0)),
        pl.BlockSpec((1,) + down_mats.shape[1:], lambda j: (j, 0, 0)),
    ]
    operands = [wanted, *blocks, in_mats, down_mats]
    aliases = {}
    if stacks is not None:
        aliases = {len(operands) + i: i for i in range(5)}
        in_specs += [pl.BlockSpec(memory_space=pl.ANY)] * 5
        operands += list(stacks)
    return pl.pallas_call(
        functools.partial(chunk_kernel, features, half, rows),
        grid=(2,),
        out_shape=[jax.ShapeDtypeStruct((chunks * many, features), B16)] * 2
        + [jax.ShapeDtypeStruct((2, chunks * many, half), B16)] * 3
        + [jax.ShapeDtypeStruct((2 * rows, features), F32), jax.ShapeDtypeStruct((2 * rows, features), B16)],
        in_specs=in_specs,
        out_specs=[wide, wide, thin, thin, thin, whole((2 * rows, features)), whole((2 * rows, features))],
        scratch_shapes=[pltpu.VMEM((many, features), F32)],
        input_output_aliases=aliases,
        cost_estimate=pl.CostEstimate(
            flops=2 * 10 * many * features * half, bytes_accessed=24 * 1024 * 1024, transcendentals=2 * many * half
        ),
        compiler_params=pltpu.CompilerParams(vmem_limit_bytes=40 * 1024 * 1024),
    )(*operands)


def dense_device(tokens, grad_out, expert_ids, gate_probs, gate_weight, up_weight, down_weight):
    rows, _ = tokens.shape
    experts = lax.axis_size("rep") * lax.axis_size("exp") // 2
    mine = (lax.axis_index("rep") * lax.axis_size("exp") + lax.axis_index("exp")) // 2

    in_own = jnp.concatenate([gate_weight[0], up_weight[0]], axis=1)
    in_mats = jnp.stack([in_own, move(in_own, OTHER_CORE)])
    down_mats = jnp.stack([down_weight[0], move(down_weight[0], OTHER_CORE)])

    chosen = expert_ids[:, :, None] == jnp.arange(experts, dtype=jnp.int32)
    dense = jnp.sum(jnp.where(chosen, gate_probs[:, :, None], 0.0), axis=1)
    high = lax.reduce_precision(dense, 8, 7)
    middle = lax.reduce_precision(dense - high, 8, 7)
    low = dense - high - middle
    terms = jnp.concatenate([high, middle, low], axis=1).astype(B16)
    pad = -terms.shape[1] % 128
    block = jnp.concatenate([tokens, grad_out, jnp.pad(terms, ((0, 0), (0, pad)))], axis=1)
    lanes = jnp.arange(3 * experts + pad, dtype=jnp.int32)
    wanted = ((lanes < 3 * experts) & (lanes % experts == mine)).astype(F32)[None]

    stacks, totals = None, []
    for step in range(4):
        own = block if step == 0 else move(block, Z_IN[step])
        first = move(own, FIRST_FLIP)
        blocks = [own, first, move(own, SECOND_FLIP), move(first, SECOND_FLIP)]
        *stacks, keep, send = chunk_call(step, 4, wanted, blocks, in_mats, down_mats, stacks)
        partial = keep + move(send, SECOND_FLIP).astype(F32)
        partial = partial[:rows] + move(partial[rows:].astype(B16), FIRST_FLIP).astype(F32)
        if step > 0:
            partial = move(partial.astype(B16), Z_BACK[step]).astype(F32)
        totals.append(partial)
    token_grad = (totals[0] + totals[1] + totals[2] + totals[3]).astype(B16)
    all_in, all_scaled, all_gate, all_up, all_hidden = stacks

    def grads(part):
        pairs = ((all_in, all_gate[part]), (all_in, all_up[part]), (all_hidden[part], all_scaled))
        return [lax.dot_general(a, b, FIRST, preferred_element_type=F32) for a, b in pairs]

    other = [value.astype(B16) for value in grads(1)]
    arrived = [move(value, OTHER_CORE) for value in other]
    summed = [(here + there.astype(F32)).astype(B16)[None] for here, there in zip(grads(0), arrived)]
    return (token_grad, *summed)


def sparse_device(tokens, grad_out, expert_ids, gate_probs, gate_weight, up_weight, down_weight):
    rep_count = lax.axis_size("rep")
    exp_count = lax.axis_size("exp")
    tok_rows, features = tokens.shape
    top_count = expert_ids.shape[1]
    experts = rep_count * exp_count // 2
    capacity = 2 * ((tok_rows * top_count // experts + 2) // 2)
    routed = tok_rows * top_count
    flat_ids = expert_ids.reshape(routed)
    order_index = jnp.arange(routed, dtype=jnp.int32)
    earlier = (flat_ids[:, None] == flat_ids[None, :]) & (
        order_index[None, :] < order_index[:, None]
    )
    slot_rank = jnp.sum(earlier.astype(jnp.int32), axis=1)
    slot_index = flat_ids * capacity + slot_rank
    slot_range = jnp.arange(experts * capacity, dtype=jnp.int32)
    selector = slot_range[:, None] == slot_index[None, :]
    select_rows = selector.astype(jnp.bfloat16)
    rows_in = jnp.repeat(tokens, top_count, axis=0)
    rows_grad = (
        (gate_probs[:, :, None] * grad_out[:, None, :].astype(jnp.float32))
        .reshape(routed, features)
        .astype(jnp.bfloat16)
    )
    packed_in = jnp.dot(select_rows, rows_in, preferred_element_type=jnp.float32).astype(
        jnp.bfloat16
    )
    packed_grad = jnp.dot(select_rows, rows_grad, preferred_element_type=jnp.float32).astype(
        jnp.bfloat16
    )
    send_in = jnp.repeat(packed_in.reshape(experts, capacity, features), 2, axis=0).reshape(
        rep_count, exp_count, capacity, features
    )
    send_grad = jnp.repeat(packed_grad.reshape(experts, capacity, features), 2, axis=0).reshape(
        rep_count, exp_count, capacity, features
    )
    recv_in, recv_grad = (
        lax.all_to_all(
            lax.all_to_all(send_in, "rep", split_axis=0, concat_axis=0, tiled=True),
            "exp",
            split_axis=1,
            concat_axis=1,
            tiled=True,
        ),
        lax.all_to_all(
            lax.all_to_all(send_grad, "rep", split_axis=0, concat_axis=0, tiled=True),
            "exp",
            split_axis=1,
            concat_axis=1,
            tiled=True,
        ),
    )
    slots = rep_count * exp_count * capacity
    slot_in = recv_in.reshape(slots, features)
    slot_grad = recv_grad.reshape(slots, features)
    gate_mat = gate_weight[0]
    up_mat = up_weight[0]
    down_mat = down_weight[0]
    contract_last = (((1,), (1,)), ((), ()))
    contract_first = (((0,), (0,)), ((), ()))
    gate_pre = jnp.dot(slot_in, gate_mat, preferred_element_type=jnp.float32)
    up_pre = jnp.dot(slot_in, up_mat, preferred_element_type=jnp.float32)
    sigmoid_gate = jax.nn.sigmoid(gate_pre)
    activated = gate_pre * sigmoid_gate
    hidden = (activated * up_pre).astype(jnp.bfloat16)
    hidden_grad = lax.dot_general(
        slot_grad, down_mat, contract_last, preferred_element_type=jnp.float32
    )
    up_in = (hidden_grad * activated).astype(jnp.bfloat16)
    gate_in = (
        hidden_grad * up_pre * sigmoid_gate * (1.0 + gate_pre * (1.0 - sigmoid_gate))
    ).astype(jnp.bfloat16)
    partial_rows = lax.dot_general(
        gate_in, gate_mat, contract_last, preferred_element_type=jnp.float32
    ) + lax.dot_general(up_in, up_mat, contract_last, preferred_element_type=jnp.float32)
    gate_grad = lax.dot_general(
        slot_in, gate_in, contract_first, preferred_element_type=jnp.float32
    ).astype(jnp.bfloat16)[None]
    up_grad = lax.dot_general(
        slot_in, up_in, contract_first, preferred_element_type=jnp.float32
    ).astype(jnp.bfloat16)[None]
    down_grad = lax.dot_general(
        hidden, slot_grad, contract_first, preferred_element_type=jnp.float32
    ).astype(jnp.bfloat16)[None]
    partial_grid = partial_rows.reshape(rep_count, exp_count, capacity, features)
    returned_grid = lax.all_to_all(
        lax.all_to_all(partial_grid, "rep", split_axis=0, concat_axis=0, tiled=True),
        "exp",
        split_axis=1,
        concat_axis=1,
        tiled=True,
    )
    returned = jnp.sum(returned_grid.reshape(experts, 2, capacity, features), axis=1).reshape(
        experts * capacity, features
    )
    routed_grads = returned[slot_index]
    token_grad = jnp.sum(routed_grads.reshape(tok_rows, top_count, features), axis=1).astype(
        jnp.bfloat16
    )
    return (token_grad, gate_grad, up_grad, down_grad)


def per_device(tokens, grad_out, expert_ids, *rest):
    experts = lax.axis_size("rep") * lax.axis_size("exp") // 2
    if lax.axis_size("rep") == 4 and lax.axis_size("exp") == 8 and 2 * expert_ids.shape[1] >= experts:
        return dense_device(tokens, grad_out, expert_ids, *rest)
    return sparse_device(tokens, grad_out, expert_ids, *rest)


def solution(mesh):
    return jax.shard_map(
        per_device,
        mesh=mesh,
        in_specs=(
            P(("rep", "exp"), None),
            P(("rep", "exp"), None),
            P(("rep", "exp"), None),
            P(("rep", "exp"), None),
            P(("rep", "exp"), None, None),
            P(("rep", "exp"), None, None),
            P(("rep", "exp"), None, None),
        ),
        out_specs=(
            P(("rep", "exp"), None),
            P(("rep", "exp"), None, None),
            P(("rep", "exp"), None, None),
            P(("rep", "exp"), None, None),
        ),
        check_vma=False,
    )
```

```python
import functools

import jax
import jax.numpy as jnp
from jax import lax
from jax.experimental import pallas as pl
from jax.experimental.pallas import tpu as pltpu
from jax.sharding import PartitionSpec as P


AXES = ("rep", "exp")


def flip_pairs(move):
    pairs = []
    for z in range(4):
        for y in range(2):
            for x in range(2):
                for c in range(2):
                    tz, ty, tx, tc = move(z, y, x, c)
                    pairs.append((((z * 2 + y) * 2 + x) * 2 + c, ((tz * 2 + ty) * 2 + tx) * 2 + tc))
    return pairs


OTHER_CORE = flip_pairs(lambda z, y, x, c: (z, y, x, 1 - c))
FIRST_FLIP = flip_pairs(lambda z, y, x, c: (z, y, 1 - x, c) if c == 0 else (z, 1 - y, x, c))
SECOND_FLIP = flip_pairs(lambda z, y, x, c: (z, 1 - y, x, c) if c == 0 else (z, y, 1 - x, c))
SHIFTS = (0, 3, 2, 1)
Z_IN = [flip_pairs(lambda z, y, x, c, s=s: ((z - s) % 4, y, x, c)) for s in SHIFTS]
Z_BACK = [flip_pairs(lambda z, y, x, c, s=s: ((z + s) % 4, y, x, c)) for s in SHIFTS]
LAST = (((1,), (1,)), ((), ()))
FIRST = (((0,), (0,)), ((), ()))
F32, B16 = jnp.float32, jnp.bfloat16


def move(value, pairs):
    return lax.ppermute(value, AXES, pairs)


def chunk_kernel(features, half, rows, *refs):
    wanted, blocks, in_mat, down_mat = refs[0], refs[1:5], refs[5], refs[6]
    rows_out, scaled_out, gate_out, up_out, hidden_out, keep, send = refs[-8:-1]
    total = refs[-1]
    step = pl.program_id(0)

    @pl.when(step == 0)
    def _():
        for i, block in enumerate(blocks):
            place = pl.ds(i * rows, rows)
            rows_out[place, :] = block[:, :features]
            terms = jnp.where(wanted[...] > 0.0, block[:, 2 * features :].astype(F32), 0.0)
            weight = jnp.sum(terms, axis=1, keepdims=True)
            scaled_out[place, :] = (weight * block[:, features : 2 * features].astype(F32)).astype(B16)

    pre = jnp.dot(rows_out[...], in_mat[0], preferred_element_type=F32)
    gate_pre, up_pre = pre[:, :half], pre[:, half:]
    hidden_grad = lax.dot_general(scaled_out[...], down_mat[0], LAST, preferred_element_type=F32)
    sigmoid_gate = jax.nn.sigmoid(gate_pre)
    activated = gate_pre * sigmoid_gate
    hidden_out[0] = (activated * up_pre).astype(B16)
    up_in = (hidden_grad * activated).astype(B16)
    gate_in = (hidden_grad * up_pre * sigmoid_gate * (1.0 + gate_pre * (1.0 - sigmoid_gate))).astype(B16)
    gate_out[0] = gate_in
    up_out[0] = up_in
    part = lax.dot_general(jnp.concatenate([gate_in, up_in], axis=1), in_mat[0], LAST, preferred_element_type=F32)

    @pl.when(step == 0)
    def _():
        total[...] = part

    @pl.when(step == 1)
    def _():
        keep[...] = total[: 2 * rows, :] + part[: 2 * rows]
        send[...] = (total[2 * rows :, :] + part[2 * rows :]).astype(B16)


def chunk_call(place, chunks, wanted, blocks, in_mats, down_mats, stacks):
    rows, width = blocks[0].shape
    features = down_mats.shape[2]
    half = down_mats.shape[1]
    many = 4 * rows
    whole = lambda shape: pl.BlockSpec(shape, lambda j: (0,) * len(shape))
    wide = pl.BlockSpec((many, features), lambda j: (place, 0))
    thin = pl.BlockSpec((1, many, half), lambda j: (j, place, 0))
    in_specs = [whole(wanted.shape)] + [whole((rows, width))] * 4 + [
        pl.BlockSpec((1,) + in_mats.shape[1:], lambda j: (j, 0, 0)),
        pl.BlockSpec((1,) + down_mats.shape[1:], lambda j: (j, 0, 0)),
    ]
    operands = [wanted, *blocks, in_mats, down_mats]
    aliases = {}
    if stacks is not None:
        aliases = {len(operands) + i: i for i in range(5)}
        in_specs += [pl.BlockSpec(memory_space=pl.ANY)] * 5
        operands += list(stacks)
    return pl.pallas_call(
        functools.partial(chunk_kernel, features, half, rows),
        grid=(2,),
        out_shape=[jax.ShapeDtypeStruct((chunks * many, features), B16)] * 2
        + [jax.ShapeDtypeStruct((2, chunks * many, half), B16)] * 3
        + [jax.ShapeDtypeStruct((2 * rows, features), F32), jax.ShapeDtypeStruct((2 * rows, features), B16)],
        in_specs=in_specs,
        out_specs=[wide, wide, thin, thin, thin, whole((2 * rows, features)), whole((2 * rows, features))],
        scratch_shapes=[pltpu.VMEM((many, features), F32)],
        input_output_aliases=aliases,
        cost_estimate=pl.CostEstimate(
            flops=2 * 10 * many * features * half, bytes_accessed=24 * 1024 * 1024, transcendentals=2 * many * half
        ),
        compiler_params=pltpu.CompilerParams(vmem_limit_bytes=40 * 1024 * 1024),
    )(*operands)


def dense_device(tokens, grad_out, expert_ids, gate_probs, gate_weight, up_weight, down_weight):
    rows, _ = tokens.shape
    experts = lax.axis_size("rep") * lax.axis_size("exp") // 2
    mine = (lax.axis_index("rep") * lax.axis_size("exp") + lax.axis_index("exp")) // 2

    in_own = jnp.concatenate([gate_weight[0], up_weight[0]], axis=1)
    in_other = move(in_own, OTHER_CORE)
    down_other = move(down_weight[0], OTHER_CORE)
    in_mats = jnp.stack([in_own, in_other])
    down_mats = jnp.stack([down_weight[0], down_other])

    chosen = expert_ids[:, :, None] == jnp.arange(experts, dtype=jnp.int32)
    dense = jnp.sum(jnp.where(chosen, gate_probs[:, :, None], 0.0), axis=1)
    high = lax.reduce_precision(dense, 8, 7)
    middle = lax.reduce_precision(dense - high, 8, 7)
    low = dense - high - middle
    terms = jnp.concatenate([high, middle, low], axis=1).astype(B16)
    pad = -terms.shape[1] % 128
    block = jnp.concatenate([tokens, grad_out, jnp.pad(terms, ((0, 0), (0, pad)))], axis=1)
    lanes = jnp.arange(3 * experts + pad, dtype=jnp.int32)
    wanted = ((lanes < 3 * experts) & (lanes % experts == mine)).astype(F32)[None]

    stacks, totals = None, []
    for step in range(4):
        own = block if step == 0 else move(block, Z_IN[step])
        first = move(own, FIRST_FLIP)
        blocks = [own, first, move(own, SECOND_FLIP), move(first, SECOND_FLIP)]
        *stacks, keep, send = chunk_call(step, 4, wanted, blocks, in_mats, down_mats, stacks)
        partial = keep + move(send, SECOND_FLIP).astype(F32)
        partial = partial[:rows] + move(partial[rows:].astype(B16), FIRST_FLIP).astype(F32)
        if step > 0:
            partial = move(partial.astype(B16), Z_BACK[step]).astype(F32)
        totals.append(partial)
    token_grad = (totals[0] + totals[1] + totals[2] + totals[3]).astype(B16)
    all_in, all_scaled, all_gate, all_up, all_hidden = stacks

    def grads(part):
        pairs = ((all_in, all_gate[part]), (all_in, all_up[part]), (all_hidden[part], all_scaled))
        return [functools.partial(lax.dot_general, a, b, FIRST, preferred_element_type=F32) for a, b in pairs]

    arrived, summed = [], []
    for other in grads(1):
        value = other().astype(B16)
        arrived.append(move(value, OTHER_CORE))
    for i, own in enumerate(grads(0)):
        summed.append((own() + arrived[i].astype(F32)).astype(B16)[None])
    return (token_grad, *summed)


def sparse_device(tokens, grad_out, expert_ids, gate_probs, gate_weight, up_weight, down_weight):
    rep_count = lax.axis_size("rep")
    exp_count = lax.axis_size("exp")
    tok_rows, features = tokens.shape
    top_count = expert_ids.shape[1]
    experts = rep_count * exp_count // 2
    capacity = 2 * ((tok_rows * top_count // experts + 2) // 2)
    routed = tok_rows * top_count
    flat_ids = expert_ids.reshape(routed)
    order_index = jnp.arange(routed, dtype=jnp.int32)
    earlier = (flat_ids[:, None] == flat_ids[None, :]) & (
        order_index[None, :] < order_index[:, None]
    )
    slot_rank = jnp.sum(earlier.astype(jnp.int32), axis=1)
    slot_index = flat_ids * capacity + slot_rank
    slot_range = jnp.arange(experts * capacity, dtype=jnp.int32)
    selector = slot_range[:, None] == slot_index[None, :]
    select_rows = selector.astype(jnp.bfloat16)
    rows_in = jnp.repeat(tokens, top_count, axis=0)
    rows_grad = (
        (gate_probs[:, :, None] * grad_out[:, None, :].astype(jnp.float32))
        .reshape(routed, features)
        .astype(jnp.bfloat16)
    )
    packed_in = jnp.dot(select_rows, rows_in, preferred_element_type=jnp.float32).astype(
        jnp.bfloat16
    )
    packed_grad = jnp.dot(select_rows, rows_grad, preferred_element_type=jnp.float32).astype(
        jnp.bfloat16
    )
    send_in = jnp.repeat(packed_in.reshape(experts, capacity, features), 2, axis=0).reshape(
        rep_count, exp_count, capacity, features
    )
    send_grad = jnp.repeat(packed_grad.reshape(experts, capacity, features), 2, axis=0).reshape(
        rep_count, exp_count, capacity, features
    )
    recv_in, recv_grad = (
        lax.all_to_all(
            lax.all_to_all(send_in, "rep", split_axis=0, concat_axis=0, tiled=True),
            "exp",
            split_axis=1,
            concat_axis=1,
            tiled=True,
        ),
        lax.all_to_all(
            lax.all_to_all(send_grad, "rep", split_axis=0, concat_axis=0, tiled=True),
            "exp",
            split_axis=1,
            concat_axis=1,
            tiled=True,
        ),
    )
    slots = rep_count * exp_count * capacity
    slot_in = recv_in.reshape(slots, features)
    slot_grad = recv_grad.reshape(slots, features)
    gate_mat = gate_weight[0]
    up_mat = up_weight[0]
    down_mat = down_weight[0]
    contract_last = (((1,), (1,)), ((), ()))
    contract_first = (((0,), (0,)), ((), ()))
    gate_pre = jnp.dot(slot_in, gate_mat, preferred_element_type=jnp.float32)
    up_pre = jnp.dot(slot_in, up_mat, preferred_element_type=jnp.float32)
    sigmoid_gate = jax.nn.sigmoid(gate_pre)
    activated = gate_pre * sigmoid_gate
    hidden = (activated * up_pre).astype(jnp.bfloat16)
    hidden_grad = lax.dot_general(
        slot_grad, down_mat, contract_last, preferred_element_type=jnp.float32
    )
    up_in = (hidden_grad * activated).astype(jnp.bfloat16)
    gate_in = (
        hidden_grad * up_pre * sigmoid_gate * (1.0 + gate_pre * (1.0 - sigmoid_gate))
    ).astype(jnp.bfloat16)
    partial_rows = lax.dot_general(
        gate_in, gate_mat, contract_last, preferred_element_type=jnp.float32
    ) + lax.dot_general(up_in, up_mat, contract_last, preferred_element_type=jnp.float32)
    gate_grad = lax.dot_general(
        slot_in, gate_in, contract_first, preferred_element_type=jnp.float32
    ).astype(jnp.bfloat16)[None]
    up_grad = lax.dot_general(
        slot_in, up_in, contract_first, preferred_element_type=jnp.float32
    ).astype(jnp.bfloat16)[None]
    down_grad = lax.dot_general(
        hidden, slot_grad, contract_first, preferred_element_type=jnp.float32
    ).astype(jnp.bfloat16)[None]
    partial_grid = partial_rows.reshape(rep_count, exp_count, capacity, features)
    returned_grid = lax.all_to_all(
        lax.all_to_all(partial_grid, "rep", split_axis=0, concat_axis=0, tiled=True),
        "exp",
        split_axis=1,
        concat_axis=1,
        tiled=True,
    )
    returned = jnp.sum(returned_grid.reshape(experts, 2, capacity, features), axis=1).reshape(
        experts * capacity, features
    )
    routed_grads = returned[slot_index]
    token_grad = jnp.sum(routed_grads.reshape(tok_rows, top_count, features), axis=1).astype(
        jnp.bfloat16
    )
    return (token_grad, gate_grad, up_grad, down_grad)


def per_device(tokens, grad_out, expert_ids, *rest):
    experts = lax.axis_size("rep") * lax.axis_size("exp") // 2
    if lax.axis_size("rep") == 4 and lax.axis_size("exp") == 8 and 2 * expert_ids.shape[1] >= experts:
        return dense_device(tokens, grad_out, expert_ids, *rest)
    return sparse_device(tokens, grad_out, expert_ids, *rest)


def solution(mesh):
    return jax.shard_map(
        per_device,
        mesh=mesh,
        in_specs=(
            P(("rep", "exp"), None),
            P(("rep", "exp"), None),
            P(("rep", "exp"), None),
            P(("rep", "exp"), None),
            P(("rep", "exp"), None, None),
            P(("rep", "exp"), None, None),
            P(("rep", "exp"), None, None),
        ),
        out_specs=(
            P(("rep", "exp"), None),
            P(("rep", "exp"), None, None),
            P(("rep", "exp"), None, None),
            P(("rep", "exp"), None, None),
        ),
        check_vma=False,
    )
```
